32 devices in a mesh: groups: 2 (over x), kv: 16 (over z, y, core).
Axes of the slice: x: 2, y: 2, z: 4, core: 2. Of those that a mesh axis runs over, the one named last changes fastest.
Arguments:
- queries: bfloat16 [2, 64, 16384], P(None, ('groups', 'kv')), parts along dimension 1, may hold values from -90 to 90
- new_kv: bfloat16 [2, 2, 64, 1024], P(None, None, ('groups', 'kv')), parts along dimension 2, may hold values from -41 to 41
- root_kv: bfloat16 [128, 2, 128, 1024], P(('groups', 'kv')), parts along dimension 0, may hold values from -24 to 24
- branch_kv: bfloat16 [128, 2, 128, 1024], P(('groups', 'kv')), parts along dimension 0, may hold values from -24 to 24
- tail_kv: bfloat16 [64, 2, 512, 1024], P(('groups', 'kv')), parts along dimension 0, may hold values from -24 to 24
- parent: int32 [98], P('groups'), parts along dimension 0, may hold values from 0 to 16, as said below
- node_len: int32 [98], P('groups'), parts along dimension 0, may hold values from 1 to 8192, as said below
- leaf_of: int32 [64], P('groups'), parts along dimension 0, may hold values from 17 to 48, as said below
- branch_slot: int32 [128], P('groups'), parts along dimension 0, may hold values from 1 to 49, as said below
Outputs:
- attended: bfloat16 [2, 64, 16384], P(None, ('groups', 'kv')), parts along dimension 1
The draws below stay inside these ranges and needn't reach their ends.
There are 2 independent parts, one for each index of `groups`. The reference program is written for one: setup_inputs(seed, part) draws one part's arguments, and reference() takes and returns one part's arrays. A program takes and returns all parts, laid end to end along the dimension named above; each array names one. Nothing has to cross between parts.
Inputs may be any that keep to these rules, and one draw needn't show every extreme that they name: Node 0 is the root and its own parent; nodes 1 to 16 are branch prefixes with parent 0; nodes 17 to 48 are private tails, each with a branch prefix as parent. At most 6 tails share a branch prefix, and some branch prefix has exactly 6. node_len[0] = 8192; a branch prefix holds 1 to 512 tokens and a tail 1 to 512; some branch prefix and some tail hold exactly those most. `leaf_of`: every tail node is the leaf of exactly one request. `branch_slot`: A branch prefix of L tokens owns exactly ceil(L / 128) slots, which hold its tokens in order of slot index, 128 to a slot, the last one partly; all other slots hold 49.
All inputs are finite; a program needn't handle non-finite values.
Results may differ from the reference program's by a relative error of at most 0.002.
Values may be sent and summed in bfloat16 or wider, within the bound.
A program may use at most 192 MiB of HBM per device.

```python
import jax
import jax.numpy as jnp
from jax import lax

QH = 128
KVH = 8
HD = 128
BLOCK = 128
ROOT_DEV = 4
BR_DEV = 4
BRANCH = 16
GROUP = 16
REQ = 32
CAP = 6
ROOT_SLOTS = 64
BR_SLOTS = 64
BR_MAX_BLOCKS = 4
TAIL_LEN = 512
NODES = 49
N_KV = 16


def tree_tables(key):
    request_ids = jnp.arange(REQ, dtype=jnp.int32)
    labels = jnp.where(request_ids < CAP, 0, 1 + (request_ids - CAP) % (BRANCH - 1)).astype(jnp.int32)
    relabel = jax.random.permutation(jax.random.fold_in(key, 1), BRANCH).astype(jnp.int32)
    leaf_branch = (1 + relabel[labels]).astype(jnp.int32)
    parent_table = jnp.concatenate([jnp.zeros((1 + BRANCH,), jnp.int32), leaf_branch])
    longest = BR_MAX_BLOCKS * BLOCK
    branch_len = jax.random.randint(jax.random.fold_in(key, 2), (BRANCH,), 1, longest + 1, dtype=jnp.int32)
    branch_len = branch_len.at[relabel[1]].set(longest)
    tail_len = jax.random.randint(jax.random.fold_in(key, 3), (REQ,), 1, TAIL_LEN + 1, dtype=jnp.int32)
    tail_len = tail_len.at[0].set(TAIL_LEN)
    length_table = jnp.concatenate([jnp.full((1,), ROOT_SLOTS * BLOCK, jnp.int32), branch_len, tail_len])
    leaf_table = (BRANCH + 1 + jax.random.permutation(jax.random.fold_in(key, 4), REQ)).astype(jnp.int32)
    block_counts = (branch_len + BLOCK - 1) // BLOCK
    block_ends = jnp.cumsum(block_counts).astype(jnp.int32)
    slot_ids = jnp.arange(BR_SLOTS, dtype=jnp.int32)
    owners = 1 + jnp.sum((slot_ids[:, None] >= block_ends[None, :]).astype(jnp.int32), axis=1)
    owners = jnp.where(slot_ids < block_ends[-1], owners, NODES).astype(jnp.int32)
    placing = jax.random.permutation(jax.random.fold_in(key, 5), BR_SLOTS)
    slot_table = jnp.zeros((BR_SLOTS,), jnp.int32).at[placing].set(owners)
    return (parent_table, length_table, leaf_table, slot_table)


def draw_parent(key, part):
    return tree_tables(key)[0]


def draw_node_len(key, part):
    return tree_tables(key)[1]


def draw_leaf_of(key, part):
    return tree_tables(key)[2]


def draw_branch_slot(key, part):
    return tree_tables(key)[3]


def base_queries(key):
    shape_all = (2, REQ, QH * HD)
    return 2.5 * jnp.clip(jax.random.normal(jax.random.fold_in(key, 11), shape_all, jnp.float32), -6.0, 6.0)


def draw_queries(key, part):
    query_all = base_queries(key)
    return query_all.astype(jnp.bfloat16)


def draw_new_kv(key, part):
    query_all = base_queries(key).reshape(2, REQ, KVH, GROUP, HD)
    noise = jnp.clip(jax.random.normal(jax.random.fold_in(key, 51), (2, REQ, KVH * HD), jnp.float32), -6.0, 6.0)
    key_rows = 2.5 * jnp.mean(query_all, axis=3).reshape(2, REQ, KVH * HD) + 0.5 * noise
    value_rows = 4.0 * jnp.clip(jax.random.normal(jax.random.fold_in(key, 52), (2, REQ, KVH * HD), jnp.float32), -6.0, 6.0)
    return jnp.stack([key_rows, value_rows], axis=1).astype(jnp.bfloat16)


def cache_blocks(key, salt, count, length):
    shape_all = (count, length, KVH * HD)
    key_rows = jnp.clip(jax.random.normal(jax.random.fold_in(key, salt), shape_all, jnp.float32), -6.0, 6.0)
    value_rows = 4.0 * jnp.clip(jax.random.normal(jax.random.fold_in(key, salt + 1), shape_all, jnp.float32), -6.0, 6.0)
    return (key_rows, value_rows)


def draw_root_kv(key, part):
    key_rows, value_rows = cache_blocks(key, 21, ROOT_SLOTS, BLOCK)
    return jnp.stack([key_rows, value_rows], axis=1).astype(jnp.bfloat16)


def draw_branch_kv(key, part):
    key_rows, value_rows = cache_blocks(key, 31, BR_SLOTS, BLOCK)
    return jnp.stack([key_rows, value_rows], axis=1).astype(jnp.bfloat16)


def draw_tail_kv(key, part):
    key_rows, value_rows = cache_blocks(key, 41, REQ, TAIL_LEN)
    return jnp.stack([key_rows, value_rows], axis=1).astype(jnp.bfloat16)


def setup_inputs(seed: int = 0, part: int = 0) -> dict:
    key_list = jax.random.split(jax.random.key(seed), 10)
    part_splits = jax.random.split(jax.random.fold_in(key_list[9], part), 10)
    queries = draw_queries(jax.random.fold_in(jax.random.fold_in(key_list[9], part), 71), part)
    new_kv = draw_new_kv(jax.random.fold_in(jax.random.fold_in(key_list[9], part), 71), part)
    root_kv = draw_root_kv(jax.random.fold_in(jax.random.fold_in(key_list[9], part), 71), part)
    branch_kv = draw_branch_kv(jax.random.fold_in(jax.random.fold_in(key_list[9], part), 71), part)
    tail_kv = draw_tail_kv(jax.random.fold_in(jax.random.fold_in(key_list[9], part), 71), part)
    parent = draw_parent(jax.random.fold_in(jax.random.fold_in(key_list[9], part), 71), part)
    node_len = draw_node_len(jax.random.fold_in(jax.random.fold_in(key_list[9], part), 71), part)
    leaf_of = draw_leaf_of(jax.random.fold_in(jax.random.fold_in(key_list[9], part), 71), part)
    branch_slot = draw_branch_slot(jax.random.fold_in(jax.random.fold_in(key_list[9], part), 71), part)
    return dict(queries=queries, new_kv=new_kv, root_kv=root_kv, branch_kv=branch_kv, tail_kv=tail_kv, parent=parent, node_len=node_len, leaf_of=leaf_of, branch_slot=branch_slot)


NEG_FILL = -1.0e30


def reference(queries, new_kv, root_kv, branch_kv, tail_kv, parent, node_len, leaf_of, branch_slot):
    slot_ids = jnp.arange(BR_SLOTS, dtype=jnp.int32)
    same_node = branch_slot[:, None] == branch_slot[None, :]
    before_slot = slot_ids[None, :] < slot_ids[:, None]
    ranks = jnp.sum((same_node & before_slot).astype(jnp.int32), axis=1)
    owner_len = node_len[jnp.minimum(branch_slot, NODES - 1)]
    filled = jnp.where(branch_slot < NODES, jnp.clip(owner_len - ranks * BLOCK, 0, BLOCK), 0)
    root_span = ROOT_DEV * BLOCK
    root_keys = root_kv[:, 0].reshape(N_KV, root_span, KVH, HD).astype(jnp.float32)
    root_values = root_kv[:, 1].reshape(N_KV, root_span, KVH, HD).astype(jnp.float32)
    scale = HD ** -0.5
    part_ids = jnp.arange(N_KV, dtype=jnp.int32)

    def one_request(request):
        leaf = leaf_of[request]
        branch = parent[leaf]
        sort_key = jnp.where(branch_slot == branch, ranks, BR_SLOTS + slot_ids).astype(jnp.int32)
        ordering = jnp.argsort(sort_key, stable=True)[:BR_MAX_BLOCKS].astype(jnp.int32)
        picked = branch_kv[ordering]
        counts = jnp.where(branch_slot[ordering] == branch, filled[ordering], 0)
        branch_keys = picked[:, 0].reshape(BR_MAX_BLOCKS * BLOCK, KVH, HD).astype(jnp.float32)
        branch_values = picked[:, 1].reshape(BR_MAX_BLOCKS * BLOCK, KVH, HD).astype(jnp.float32)
        branch_live = (jnp.arange(BLOCK, dtype=jnp.int32)[None, :] < counts[:, None]).reshape(-1)
        token_part = jnp.repeat((ordering // BR_DEV).astype(jnp.int32), BLOCK)
        onehot = (token_part[:, None] == part_ids[None, :]) & branch_live[:, None]
        onehot_float = onehot.astype(jnp.float32)
        tail_keys = tail_kv[request, 0].reshape(TAIL_LEN, KVH, HD).astype(jnp.float32)
        tail_values = tail_kv[request, 1].reshape(TAIL_LEN, KVH, HD).astype(jnp.float32)
        tail_live = jnp.arange(TAIL_LEN, dtype=jnp.int32) < node_len[leaf]
        fresh_keys = new_kv[:, 0, request].reshape(2, KVH, HD).astype(jnp.float32)
        fresh_values = new_kv[:, 1, request].reshape(2, KVH, HD).astype(jnp.float32)
        own_keys = jnp.concatenate([tail_keys, fresh_keys], axis=0)
        own_values = jnp.concatenate([tail_values, fresh_values], axis=0)
        results = []
        for step_index in range(2):
            query_rows = queries[step_index, request].reshape(KVH, GROUP, HD).astype(jnp.float32)
            root_scores = jnp.einsum("kgd,ntkd->kgnt", query_rows, root_keys, precision=lax.Precision.HIGHEST) * scale
            branch_scores = jnp.einsum("kgd,tkd->kgt", query_rows, branch_keys, precision=lax.Precision.HIGHEST) * scale
            branch_scores = jnp.where(branch_live[None, None, :], branch_scores, NEG_FILL)
            root_peak = jnp.max(root_scores, axis=-1)
            branch_peak = jnp.max(jnp.where(onehot[None, None], branch_scores[..., None], NEG_FILL), axis=2)
            part_peak = jnp.maximum(root_peak, branch_peak)
            root_weights = jnp.exp(root_scores - part_peak[..., None])
            token_peak = part_peak[:, :, jnp.minimum(token_part, N_KV - 1)]
            branch_weights = jnp.where(branch_live[None, None, :], jnp.exp(branch_scores - token_peak), 0.0)
            part_totals = jnp.sum(root_weights, axis=-1) + jnp.einsum("kgt,tn->kgn", branch_weights, onehot_float, precision=lax.Precision.HIGHEST)
            root_rounded = lax.optimization_barrier(root_weights.astype(jnp.bfloat16)).astype(jnp.float32)
            branch_rounded = lax.optimization_barrier(branch_weights.astype(jnp.bfloat16)).astype(jnp.float32)
            part_out = jnp.einsum("kgnt,ntkd->kgnd", root_rounded, root_values, precision=lax.Precision.HIGHEST)
            spread = branch_rounded[..., None] * onehot_float[None, None]
            part_out = part_out + jnp.einsum("kgtn,tkd->kgnd", spread, branch_values, precision=lax.Precision.HIGHEST)
            normed = part_out / part_totals[..., None]
            normed = lax.optimization_barrier(normed.astype(jnp.bfloat16)).astype(jnp.float32)
            own_live = jnp.concatenate([tail_live, jnp.arange(2, dtype=jnp.int32) <= step_index])
            own_scores = jnp.einsum("kgd,tkd->kgt", query_rows, own_keys, precision=lax.Precision.HIGHEST) * scale
            own_scores = jnp.where(own_live[None, None, :], own_scores, NEG_FILL)
            own_peak = jnp.max(own_scores, axis=-1)
            own_weights = jnp.where(own_live[None, None, :], jnp.exp(own_scores - own_peak[..., None]), 0.0)
            own_total = jnp.sum(own_weights, axis=-1)
            own_rounded = lax.optimization_barrier(own_weights.astype(jnp.bfloat16)).astype(jnp.float32)
            own_out = jnp.einsum("kgt,tkd->kgd", own_rounded, own_values, precision=lax.Precision.HIGHEST)
            top = jnp.maximum(jnp.max(part_peak, axis=-1), own_peak)
            part_factor = part_totals * jnp.exp(part_peak - top[..., None])
            own_factor = jnp.exp(own_peak - top)
            numer = jnp.sum(part_factor[..., None] * normed, axis=2) + own_factor[..., None] * own_out
            denom = jnp.sum(part_factor, axis=-1) + own_factor * own_total
            outputs = numer / denom[..., None]
            results.append(outputs.reshape(QH * HD).astype(jnp.bfloat16))
        return jnp.stack(results)

    gathered = lax.map(one_request, jnp.arange(REQ, dtype=jnp.int32))
    return jnp.swapaxes(gathered, 0, 1)
```

```python
import functools

import jax
import jax.numpy as jnp
from jax import lax
from jax.experimental import pallas as pl
from jax.experimental.pallas import tpu as pltpu
from jax.sharding import PartitionSpec as P

QH = 128
KVH = 8
HD = 128
PAIR = 2
MASKED = -1e30
LOG2E = 1.4426950408889634


def attend(scores):
    unit = HD**-0.5 * LOG2E
    top = functools.reduce(jnp.maximum, [jnp.max(s, axis=0, keepdims=True) for s in scores]) * unit
    weights = [jnp.exp2(s * unit - top) for s in scores]
    total = functools.reduce(jnp.add, [jnp.sum(w, axis=0, keepdims=True) for w in weights])
    return top, total, [w.astype(jnp.bfloat16) for w in weights]


def matmul(a, b, dims):
    return lax.dot_general(a, b, (dims, ((), ())), preferred_element_type=jnp.float32)


def merge(stat_a, out_a, stat_b, out_b):
    top = jnp.maximum(stat_a[0:1], stat_b[0:1])
    wa = stat_a[1:2] * jnp.exp2(stat_a[0:1] - top)
    wb = stat_b[1:2] * jnp.exp2(stat_b[0:1] - top)
    total = wa + wb
    inv = 1.0 / total
    out = out_a.astype(jnp.float32) * (wa * inv) + out_b.astype(jnp.float32) * (wb * inv)
    return jnp.concatenate([top, total], axis=0), out


def kernel(
    devices, rows, req_here,
    q_ref, lim_ref, tl_ref, new_ref, root_hbm, branch_hbm, tail_hbm,
    out_ref,
    qbuf, root, branch, tail, vt,
    o1, s1, r1, t1, o2, s2, r2, t2, o3, s3, r3, t3, tacc, tst,
    hbm_sem, agz_s, agz_r, agy_s, agy_r, agc_s, agc_r,
    c_s, c_r, y_s, y_r, z_s, z_r,
):
    depth = devices // 4
    chunks = KVH // PAIR
    me = lax.axis_index("kv")
    core = lax.rem(me, 2)
    yy = lax.rem(me // 2, 2)
    zz = me // 4
    core_peer = me + 1 - 2 * core
    y_peer = me + 2 - 4 * yy
    n_root = root.shape[0]
    n_branch = branch.shape[0]
    quarter = depth * rows

    def z_peer(offset):
        z = lax.rem(zz + offset, depth)
        return z, z * 4 + yy * 2 + core

    loads = [
        pltpu.make_async_copy(tail_hbm, tail, hbm_sem.at[0]),
        pltpu.make_async_copy(root_hbm, root, hbm_sem.at[1]),
        pltpu.make_async_copy(branch_hbm, branch, hbm_sem.at[2]),
    ]
    for load in loads:
        load.start()

    barrier = pltpu.get_barrier_semaphore()
    for peer in [core_peer, y_peer] + [z_peer(o)[1] for o in range(1, depth)]:
        pl.semaphore_signal(
            barrier, inc=1, device_id={"kv": peer}, device_id_type=pl.DeviceIdType.MESH
        )
    pl.semaphore_wait(barrier, depth + 1)

    def remote(src, dst, send, recv, peer):
        return pltpu.make_async_remote_copy(
            src_ref=src, dst_ref=dst, send_sem=send, recv_sem=recv,
            device_id={"kv": peer}, device_id_type=pl.DeviceIdType.MESH,
        )

    def gather_z(c, o):
        return remote(
            q_ref.at[c], qbuf.at[c, core, yy, zz], agz_s.at[c, o], agz_r.at[c, o], z_peer(o)[1]
        )

    def gather_z_in(c, o):
        z = lax.rem(zz + depth - o, depth)
        return remote(
            q_ref.at[c], qbuf.at[c, core, yy, z], agz_s.at[c, o], agz_r.at[c, o], z_peer(o)[1]
        )

    def gather_y(c, y):
        return remote(qbuf.at[c, core, yy], qbuf.at[c, core, y], agy_s.at[c], agy_r.at[c], y_peer)

    def gather_c(c, half):
        return remote(qbuf.at[c, core], qbuf.at[c, half], agc_s.at[c], agc_r.at[c], core_peer)

    def send_c(c):
        return (
            remote(o1.at[c, 1 - core], r1.at[c], c_s.at[c, 0], c_r.at[c, 0], core_peer),
            remote(s1.at[c, 1 - core], t1.at[c], c_s.at[c, 1], c_r.at[c, 1], core_peer),
        )

    def send_y(c):
        return (
            remote(o2.at[c, 1 - yy], r2.at[c], y_s.at[c, 0], y_r.at[c, 0], y_peer),
            remote(s2.at[c, 1 - yy], t2.at[c], y_s.at[c, 1], y_r.at[c, 1], y_peer),
        )

    def send_z(c, o):
        z, peer = z_peer(o)
        return (
            remote(o3.at[c, z], r3.at[c, o], z_s.at[c, o, 0], z_r.at[c, o, 0], peer),
            remote(s3.at[c, z], t3.at[c, o], z_s.at[c, o, 1], z_r.at[c, o, 1], peer),
        )

    @pl.loop(0, chunks)
    def _(c):
        for o in range(1, depth):
            gather_z(c, o).start()
        qbuf[c, core, yy, zz] = q_ref[c]

    for load in loads:
        load.wait()

    def head_cols(k):
        return pl.ds(pl.multiple_of(k * HD, HD), HD)

    def tail_part(c):
        lanes = PAIR * rows
        left = lax.broadcasted_iota(jnp.int32, (1, lanes), 1) < rows
        query = [q_ref[c, h] for h in range(PAIR)]
        cols = [head_cols(c * PAIR + h) for h in range(PAIR)]
        scores = []
        for r in range(req_here):
            s = jnp.concatenate(
                [matmul(tail[r, 0, :, cols[h]], query[h], ((1,), (1,))) for h in range(PAIR)], axis=1
            )
            token = lax.broadcasted_iota(jnp.int32, s.shape, 0)
            scores.append(jnp.where(token < tl_ref[r : r + 1, :], s, MASKED))
        s = jnp.concatenate(
            [matmul(new_ref[0, :, cols[h]], query[h], ((1,), (1,))) for h in range(PAIR)], axis=1
        )
        token = lax.broadcasted_iota(jnp.int32, s.shape, 0)
        lane = lax.broadcasted_iota(jnp.int32, s.shape, 1)
        lane_req = (lane // 16) % req_here
        lane_step = (lane // (16 * req_here)) % 2
        live = (token < 2 * req_here) & (token % req_here == lane_req)
        live = live & (token // req_here <= lane_step)
        scores.append(jnp.where(live, s, MASKED))
        top, total, weights = attend(scores)
        outs = []
        for h in range(PAIR):
            values = [tail[r, 1, :, cols[h]] for r in range(req_here)] + [new_ref[1, :, cols[h]]]
            outs.append(
                functools.reduce(
                    jnp.add, [matmul(v, w, ((0,), (0,))) for v, w in zip(values, weights)]
                )
            )
        tacc[c] = jnp.where(left, outs[0], outs[1])
        tst[c] = jnp.concatenate([top, total], axis=0)

    def cache_part(c, half):
        @pl.loop(0, PAIR * 2)
        def _(i):
            h, y = i // 2, lax.rem(i, 2)
            k = c * PAIR + h
            cols = head_cols(k)
            query = qbuf[c, half, y, :, h].reshape(quarter, HD)
            scores = [matmul(root[b, 0, :, cols], query, ((1,), (1,))) for b in range(n_root)]
            for b in range(n_branch):
                s = matmul(branch[b, 0, :, cols], query, ((1,), (1,)))
                token = lax.broadcasted_iota(jnp.int32, s.shape, 0)
                scores.append(jnp.where(token < lim_ref[half, y, b : b + 1, :], s, MASKED))
            top, total, weights = attend(scores)
            out = matmul(vt[k], jnp.concatenate(weights, axis=0), ((1,), (0,)))
            o1[c, half, h, y] = (out * (1.0 / total)).astype(jnp.bfloat16)
            s1[c, half, h, y] = jnp.concatenate([top, total], axis=0)

    @pl.loop(0, KVH)
    def _(k):
        cols = head_cols(k)
        for b in range(n_root):
            vt[k, :, b * HD : (b + 1) * HD] = root[b, 1, :, cols].T
        for b in range(n_branch):
            vt[k, :, (n_root + b) * HD : (n_root + b + 1) * HD] = branch[b, 1, :, cols].T

    @pl.loop(0, chunks + 5)
    def _(t):
        @pl.when(t < chunks)
        def _():
            for o in range(1, depth):
                gather_z_in(t, o).wait_recv()
            gather_y(t, yy).start()

        @pl.when((t >= 1) & (t < chunks + 1))
        def _():
            c = t - 1
            gather_y(c, 1 - yy).wait_recv()
            gather_c(c, core).start()

        @pl.when(t < chunks // 2)
        def _():
            tail_part(2 * t)
            tail_part(2 * t + 1)

        @pl.when((t >= 2) & (t < chunks + 2))
        def _():
            c = t - 2
            gather_c(c, 1 - core).wait_recv()
            cache_part(c, 1 - core)
            for copy in send_c(c):
                copy.start()
            cache_part(c, core)

        @pl.when((t >= 3) & (t < chunks + 3))
        def _():
            c = t - 3
            for copy in send_c(c):
                copy.wait_recv()
            for y in range(2):
                for h in range(PAIR):
                    stat, out = merge(s1[c, core, h, y], o1[c, core, h, y], t1[c, h, y], r1[c, h, y])
                    o2[c, y, h] = out.astype(jnp.bfloat16)
                    s2[c, y, h] = stat
            for copy in send_y(c):
                copy.start()

        @pl.when((t >= 4) & (t < chunks + 4))
        def _():
            c = t - 4
            for copy in send_y(c):
                copy.wait_recv()
            joined = [merge(s2[c, yy, h], o2[c, yy, h], t2[c, h], r2[c, h]) for h in range(PAIR)]
            for z in range(depth):
                part = slice(z * rows, (z + 1) * rows)
                o3[c, z] = jnp.concatenate([j[1][:, part] for j in joined], axis=1).astype(
                    jnp.bfloat16
                )
                s3[c, z] = jnp.concatenate([j[0][:, part] for j in joined], axis=1)
            for o in range(1, depth):
                for copy in send_z(c, o):
                    copy.start()

        @pl.when(t >= 5)
        def _():
            c = t - 5
            for o in range(1, depth):
                for copy in send_z(c, o):
                    copy.wait_recv()
            stats = [s3[c, zz]] + [t3[c, o] for o in range(1, depth)]
            outs = [o3[c, zz]] + [r3[c, o] for o in range(1, depth)]
            own = tst[c]
            top = functools.reduce(jnp.maximum, [s[0:1] for s in stats] + [own[0:1]])
            scale = jnp.exp2(own[0:1] - top)
            number = tacc[c] * scale
            total = own[1:2] * scale
            for s, o in zip(stats, outs):
                factor = s[1:2] * jnp.exp2(s[0:1] - top)
                number = number + o.astype(jnp.float32) * factor
                total = total + factor
            out_ref[c] = (number / total).T.astype(jnp.bfloat16)

    @pl.loop(0, chunks)
    def _(c):
        for o in range(1, depth):
            gather_z(c, o).wait_send()
            for copy in send_z(c, o):
                copy.wait_send()
        gather_y(c, yy).wait_send()
        gather_c(c, core).wait_send()
        for copy in send_c(c) + send_y(c):
            copy.wait_send()


def body(queries, new_kv, root_kv, branch_kv, tail_kv, parent, node_len, leaf_of, branch_slot):
    devices = lax.axis_size("kv")
    device_index = lax.axis_index("kv")
    steps, req_here, _ = queries.shape
    requests = req_here * devices
    group = QH // KVH
    rows = steps * req_here * group
    depth = devices // 4
    quarter = depth * rows
    chunks = KVH // PAIR
    node_count = node_len.shape[0]
    slot_count = branch_slot.shape[0]
    slots_here = branch_kv.shape[0]
    block_len = branch_kv.shape[2]

    nodes = jnp.arange(node_count, dtype=jnp.int32)
    slot_ids = jnp.arange(slot_count, dtype=jnp.int32)
    local_slots = device_index * slots_here + jnp.arange(slots_here, dtype=jnp.int32)
    local_node = lax.dynamic_slice(branch_slot, (device_index * slots_here,), (slots_here,))
    before = slot_ids[None, :] < local_slots[:, None]
    ranks = jnp.sum(((branch_slot[None, :] == local_node[:, None]) & before).astype(jnp.int32), axis=1)
    owner_len = jnp.sum(jnp.where(nodes[None, :] == local_node[:, None], node_len[None, :], 0), axis=1)
    fill = jnp.clip(owner_len - ranks * block_len, 0, block_len)
    leaf_hot = leaf_of[:, None] == nodes[None, :]
    request_branch = jnp.sum(jnp.where(leaf_hot, parent[None, :], 0), axis=1)
    request_tail = jnp.sum(jnp.where(leaf_hot, node_len[None, :], 0), axis=1)
    limit = jnp.where(request_branch[None, :] == local_node[:, None], fill[:, None], 0)
    limit = limit.reshape(slots_here, depth, 2, 2, 1, req_here, 1)
    limit = jnp.broadcast_to(limit, (slots_here, depth, 2, 2, steps, req_here, group))
    limit = jnp.transpose(limit, (3, 2, 0, 1, 4, 5, 6)).reshape(2, 2, slots_here, quarter)
    own_tail = lax.dynamic_slice(request_tail, (device_index * req_here,), (req_here,))
    lane_req = (jnp.arange(PAIR * rows, dtype=jnp.int32) // group) % req_here
    tail_limit = jnp.where(
        lane_req[None, :] == jnp.arange(req_here, dtype=jnp.int32)[:, None], own_tail[:, None], 0
    )

    query = queries.reshape(steps, req_here, KVH, group, HD)
    query = jnp.transpose(query, (2, 0, 1, 3, 4)).reshape(chunks, PAIR, rows, HD)
    fresh = jnp.swapaxes(new_kv, 0, 1).reshape(2, steps * req_here, KVH * HD)
    fresh = jnp.pad(fresh, ((0, 0), (0, 16 - steps * req_here), (0, 0)))

    bf, f32 = jnp.bfloat16, jnp.float32
    vmem = pl.BlockSpec(memory_space=pltpu.VMEM)
    hbm = pl.BlockSpec(memory_space=pl.ANY)
    lanes = PAIR * rows
    tokens = (root_kv.shape[0] + slots_here) * block_len
    dma = pltpu.SemaphoreType.DMA
    out = pl.pallas_call(
        functools.partial(kernel, devices, rows, req_here),
        out_shape=jax.ShapeDtypeStruct((chunks, lanes, HD), bf),
        in_specs=[vmem] * 4 + [hbm] * 3,
        out_specs=vmem,
        scratch_shapes=[
            pltpu.VMEM((chunks, 2, 2, depth, PAIR, rows, HD), bf),
            pltpu.VMEM(root_kv.shape, bf),
            pltpu.VMEM(branch_kv.shape, bf),
            pltpu.VMEM(tail_kv.shape, bf),
            pltpu.VMEM((KVH, HD, tokens), bf),
            pltpu.VMEM((chunks, 2, PAIR, 2, HD, quarter), bf),
            pltpu.VMEM((chunks, 2, PAIR, 2, 2, quarter), f32),
            pltpu.VMEM((chunks, PAIR, 2, HD, quarter), bf),
            pltpu.VMEM((chunks, PAIR, 2, 2, quarter), f32),
            pltpu.VMEM((chunks, 2, PAIR, HD, quarter), bf),
            pltpu.VMEM((chunks, 2, PAIR, 2, quarter), f32),
            pltpu.VMEM((chunks, PAIR, HD, quarter), bf),
            pltpu.VMEM((chunks, PAIR, 2, quarter), f32),
            pltpu.VMEM((chunks, depth, HD, lanes), bf),
            pltpu.VMEM((chunks, depth, 2, lanes), f32),
            pltpu.VMEM((chunks, depth, HD, lanes), bf),
            pltpu.VMEM((chunks, depth, 2, lanes), f32),
            pltpu.VMEM((chunks, HD, lanes), f32),
            pltpu.VMEM((chunks, 2, lanes), f32),
            dma((3,)),
            dma((chunks, depth)), dma((chunks, depth)),
            dma((chunks,)), dma((chunks,)), dma((chunks,)), dma((chunks,)),
            dma((chunks, 2)), dma((chunks, 2)), dma((chunks, 2)), dma((chunks, 2)),
            dma((chunks, depth, 2)), dma((chunks, depth, 2)),
        ],
        compiler_params=pltpu.CompilerParams(
            collective_id=0, has_side_effects=True, vmem_limit_bytes=56 * 1024 * 1024
        ),
    )(query, limit, tail_limit, fresh, root_kv, branch_kv, tail_kv)
    out = out.reshape(KVH, steps, req_here, group, HD)
    return jnp.transpose(out, (1, 2, 0, 3, 4)).reshape(steps, req_here, QH * HD)


def solution(mesh):
    return jax.shard_map(
        body,
        mesh=mesh,
        in_specs=(
            P(None, ("groups", "kv"), None),
            P(None, None, ("groups", "kv"), None),
            P(("groups", "kv"), None, None, None),
            P(("groups", "kv"), None, None, None),
            P(("groups", "kv"), None, None, None),
            P("groups"),
            P("groups"),
            P("groups"),
            P("groups"),
        ),
        out_specs=P(None, ("groups", "kv"), None),
        check_vma=False,
    )
```

```python
import functools

import jax
import jax.numpy as jnp
from jax import lax
from jax.experimental import pallas as pl
from jax.experimental.pallas import tpu as pltpu
from jax.sharding import PartitionSpec as P

QH = 128
KVH = 8
HD = 128
PAIR = 2
MASKED = -1e30
LOG2E = 1.4426950408889634


def attend(scores):
    unit = HD**-0.5 * LOG2E
    top = functools.reduce(jnp.maximum, [jnp.max(s, axis=0, keepdims=True) for s in scores]) * unit
    weights = [jnp.exp2(s * unit - top) for s in scores]
    total = functools.reduce(jnp.add, [jnp.sum(w, axis=0, keepdims=True) for w in weights])
    return top, total, [w.astype(jnp.bfloat16) for w in weights]


def matmul(a, b, dims):
    return lax.dot_general(a, b, (dims, ((), ())), preferred_element_type=jnp.float32)


def merge(stat_a, out_a, stat_b, out_b):
    top = jnp.maximum(stat_a[0:1], stat_b[0:1])
    wa = stat_a[1:2] * jnp.exp2(stat_a[0:1] - top)
    wb = stat_b[1:2] * jnp.exp2(stat_b[0:1] - top)
    total = wa + wb
    inv = 1.0 / total
    out = out_a.astype(jnp.float32) * (wa * inv) + out_b.astype(jnp.float32) * (wb * inv)
    return jnp.concatenate([top, total], axis=0), out


def kernel(
    devices, rows, req_here,
    parent, node_len, leaf_of, branch_slot,
    q_ref, new_ref, root_hbm, branch_hbm, tail_hbm,
    out_ref,
    qbuf, root, branch, tail, vt, lim_ref, tl_ref, fresh,
    o1, s1, r1, t1, o2, s2, r2, t2, o3, s3, r3, t3, tacc, tst,
    hbm_sem, agz_s, agz_r, agy_s, agy_r, agc_s, agc_r,
    c_s, c_r, y_s, y_r, z_s, z_r,
):
    depth = devices // 4
    chunks = KVH
    half_dim = HD // 2
    group = QH // KVH
    me = lax.axis_index("kv")
    core = lax.rem(me, 2)
    yy = lax.rem(me // 2, 2)
    zz = me // 4
    core_peer = me + 1 - 2 * core
    y_peer = me + 2 - 4 * yy
    n_root = root.shape[0]
    n_branch = branch.shape[0]
    quarter = depth * rows

    def z_peer(offset):
        z = lax.rem(zz + offset, depth)
        return z, z * 4 + yy * 2 + core

    loads = [
        pltpu.make_async_copy(tail_hbm, tail, hbm_sem.at[0]),
        pltpu.make_async_copy(root_hbm, root, hbm_sem.at[1]),
        pltpu.make_async_copy(branch_hbm, branch, hbm_sem.at[2]),
    ]
    for load in loads:
        load.start()

    barrier = pltpu.get_barrier_semaphore()
    for peer in [core_peer, y_peer] + [z_peer(o)[1] for o in range(1, depth)]:
        pl.semaphore_signal(
            barrier, inc=1, device_id={"kv": peer}, device_id_type=pl.DeviceIdType.MESH
        )
    pl.semaphore_wait(barrier, depth + 1)

    def remote(src, dst, send, recv, peer):
        return pltpu.make_async_remote_copy(
            src_ref=src, dst_ref=dst, send_sem=send, recv_sem=recv,
            device_id={"kv": peer}, device_id_type=pl.DeviceIdType.MESH,
        )

    def gather_z(c, o):
        return remote(
            q_ref.at[c], qbuf.at[c, core, yy, zz], agz_s.at[c, o], agz_r.at[c, o], z_peer(o)[1]
        )

    def gather_z_in(c, o):
        z = lax.rem(zz + depth - o, depth)
        return remote(
            q_ref.at[c], qbuf.at[c, core, yy, z], agz_s.at[c, o], agz_r.at[c, o], z_peer(o)[1]
        )

    def gather_y(c, y):
        return remote(qbuf.at[c, core, yy], qbuf.at[c, core, y], agy_s.at[c], agy_r.at[c], y_peer)

    def gather_c(c, half):
        return remote(qbuf.at[c, core], qbuf.at[c, half], agc_s.at[c], agc_r.at[c], core_peer)

    def send_c(c):
        return (
            remote(o1.at[c, 1 - core], r1.at[c], c_s.at[c, 0], c_r.at[c, 0], core_peer),
            remote(s1.at[c, 1 - core], t1.at[c], c_s.at[c, 1], c_r.at[c, 1], core_peer),
        )

    def send_y(c):
        return (
            remote(o2.at[c, 1 - yy], r2.at[c], y_s.at[c, 0], y_r.at[c, 0], y_peer),
            remote(s2.at[c, 1 - yy], t2.at[c], y_s.at[c, 1], y_r.at[c, 1], y_peer),
        )

    def send_z(c, o):
        z, peer = z_peer(o)
        return (
            remote(o3.at[c, z], r3.at[c, o], z_s.at[c, o, 0], z_r.at[c, o, 0], peer),
            remote(s3.at[c, z], t3.at[c, o], z_s.at[c, o, 1], z_r.at[c, o, 1], peer),
        )

    @pl.loop(0, chunks)
    def _(c):
        for o in range(1, depth):
            gather_z(c, o).start()
        qbuf[c, core, yy, zz] = q_ref[c]

    block_len = root.shape[2]
    first_slot = me * n_branch
    slot_nodes = [branch_slot[first_slot + j] for j in range(n_branch)]

    def count_rank(i, ranks):
        node = branch_slot[i]
        return tuple(
            rank + jnp.where((node == slot_nodes[j]) & (i < first_slot + j), 1, 0)
            for j, rank in enumerate(ranks)
        )

    ranks = lax.fori_loop(
        0, branch_slot.shape[0], count_rank, (jnp.int32(0),) * n_branch
    )
    fills = []
    for j in range(n_branch):
        owned = node_len[jnp.minimum(slot_nodes[j], node_len.shape[0] - 1)]
        fill = jnp.clip(owned - ranks[j] * block_len, 0, block_len)
        fills.append(jnp.where(slot_nodes[j] < node_len.shape[0], fill, 0))
    lane = lax.broadcasted_iota(jnp.int32, (1, quarter), 1)
    lane_owner = (lane // rows) * req_here + (lane // group) % req_here
    for half in range(2):
        for y in range(2):
            lane_branch = jnp.zeros((1, quarter), jnp.int32)
            for z in range(depth):
                for r in range(req_here):
                    request = ((z * 2 + y) * 2 + half) * req_here + r
                    lane_branch = jnp.where(
                        lane_owner == z * req_here + r, parent[leaf_of[request]], lane_branch
                    )
            for j in range(n_branch):
                lim_ref[half, y, j : j + 1, :] = jnp.where(
                    lane_branch == slot_nodes[j], fills[j], 0
                )
    lane = lax.broadcasted_iota(jnp.int32, (1, PAIR * rows), 1)
    for r in range(req_here):
        tl_ref[r : r + 1, :] = jnp.where(
            (lane // group) % req_here == r, node_len[leaf_of[me * req_here + r]], 0
        )
    steps = new_ref.shape[0]
    fresh[...] = jnp.zeros_like(fresh)
    for s in range(steps):
        for kv in range(2):
            fresh[kv, s * req_here : (s + 1) * req_here, :] = new_ref[s, kv]

    for load in loads:
        load.wait()

    def head_cols(k):
        return pl.ds(pl.multiple_of(k * HD, HD), HD)

    def fold(x, part):
        return jnp.concatenate([x[:half_dim, part], x[half_dim:, part]], axis=1)

    def tail_part(c):
        query = [q_ref[c * PAIR + h] for h in range(PAIR)]
        cols = [head_cols(c * PAIR + h) for h in range(PAIR)]
        scores = []
        for r in range(req_here):
            s = jnp.concatenate(
                [matmul(tail[r, 0, :, cols[h]], query[h], ((1,), (1,))) for h in range(PAIR)], axis=1
            )
            token = lax.broadcasted_iota(jnp.int32, s.shape, 0)
            scores.append(jnp.where(token < tl_ref[r : r + 1, :], s, MASKED))
        s = jnp.concatenate(
            [matmul(fresh[0, :, cols[h]], query[h], ((1,), (1,))) for h in range(PAIR)], axis=1
        )
        token = lax.broadcasted_iota(jnp.int32, s.shape, 0)
        lane = lax.broadcasted_iota(jnp.int32, s.shape, 1)
        lane_req = (lane // group) % req_here
        lane_step = (lane // (group * req_here)) % steps
        live = (token < steps * req_here) & (token % req_here == lane_req)
        live = live & (token // req_here <= lane_step)
        scores.append(jnp.where(live, s, MASKED))
        top, total, weights = attend(scores)
        outs = []
        for h in range(PAIR):
            values = [tail[r, 1, :, cols[h]] for r in range(req_here)] + [fresh[1, :, cols[h]]]
            outs.append(
                functools.reduce(
                    jnp.add, [matmul(v, w, ((0,), (0,))) for v, w in zip(values, weights)]
                )
            )
        stat = jnp.concatenate([top, total], axis=0)
        for h in range(PAIR):
            part = slice(h * rows, (h + 1) * rows)
            tacc[c * PAIR + h] = fold(outs[h], part)
            tst[c * PAIR + h] = jnp.concatenate([stat[:, part]] * 2, axis=1)

    def cache_part(c, half):
        @pl.loop(0, 2)
        def _(y):
            cols = head_cols(c)
            query = qbuf[c, half, y].reshape(quarter, HD)
            scores = [matmul(root[b, 0, :, cols], query, ((1,), (1,))) for b in range(n_root)]
            for b in range(n_branch):
                s = matmul(branch[b, 0, :, cols], query, ((1,), (1,)))
                token = lax.broadcasted_iota(jnp.int32, s.shape, 0)
                scores.append(jnp.where(token < lim_ref[half, y, b : b + 1, :], s, MASKED))
            top, total, weights = attend(scores)
            out = matmul(vt[c], jnp.concatenate(weights, axis=0), ((1,), (0,)))
            o1[c, half, y] = (out * (1.0 / total)).astype(jnp.bfloat16)
            s1[c, half, y] = jnp.concatenate([top, total], axis=0)

    @pl.loop(0, KVH)
    def _(k):
        cols = head_cols(k)
        for b in range(n_root):
            vt[k, :, b * HD : (b + 1) * HD] = root[b, 1, :, cols].T
        for b in range(n_branch):
            vt[k, :, (n_root + b) * HD : (n_root + b + 1) * HD] = branch[b, 1, :, cols].T

    @pl.loop(0, chunks + 5)
    def _(t):
        @pl.when(t < chunks)
        def _():
            for o in range(1, depth):
                gather_z_in(t, o).wait_recv()
            gather_y(t, yy).start()

        @pl.when((t >= 1) & (t < chunks + 1))
        def _():
            c = t - 1
            gather_y(c, 1 - yy).wait_recv()
            gather_c(c, core).start()

        @pl.when(t < chunks // PAIR)
        def _():
            tail_part(t)

        @pl.when((t >= 2) & (t < chunks + 2))
        def _():
            c = t - 2
            gather_c(c, 1 - core).wait_recv()
            cache_part(c, 1 - core)
            for copy in send_c(c):
                copy.start()
            cache_part(c, core)

        @pl.when((t >= 3) & (t < chunks + 3))
        def _():
            c = t - 3
            for copy in send_c(c):
                copy.wait_recv()
            for y in range(2):
                stat, out = merge(s1[c, core, y], o1[c, core, y], t1[c, y], r1[c, y])
                o2[c, y] = out.astype(jnp.bfloat16)
                s2[c, y] = stat
            for copy in send_y(c):
                copy.start()

        @pl.when((t >= 4) & (t < chunks + 4))
        def _():
            c = t - 4
            for copy in send_y(c):
                copy.wait_recv()
            stat, out = merge(s2[c, yy], o2[c, yy], t2[c], r2[c])
            for z in range(depth):
                part = slice(z * rows, (z + 1) * rows)
                o3[c, z] = fold(out, part).astype(jnp.bfloat16)
                s3[c, z] = jnp.concatenate([stat[:, part]] * 2, axis=1)
            for o in range(1, depth):
                for copy in send_z(c, o):
                    copy.start()

        @pl.when(t >= 5)
        def _():
            c = t - 5
            for o in range(1, depth):
                for copy in send_z(c, o):
                    copy.wait_recv()
            stats = [s3[c, zz]] + [t3[c, o] for o in range(1, depth)]
            outs = [o3[c, zz]] + [r3[c, o] for o in range(1, depth)]
            own = tst[c]
            top = functools.reduce(jnp.maximum, [s[0:1] for s in stats] + [own[0:1]])
            scale = jnp.exp2(own[0:1] - top)
            number = tacc[c] * scale
            total = own[1:2] * scale
            for s, o in zip(stats, outs):
                factor = s[1:2] * jnp.exp2(s[0:1] - top)
                number = number + o.astype(jnp.float32) * factor
                total = total + factor
            out = number / total
            out = jnp.concatenate([out[:, :rows], out[:, rows:]], axis=0)
            out_ref[c] = out.T.astype(jnp.bfloat16)

    @pl.loop(0, chunks)
    def _(c):
        for o in range(1, depth):
            gather_z(c, o).wait_send()
            for copy in send_z(c, o):
                copy.wait_send()
        gather_y(c, yy).wait_send()
        gather_c(c, core).wait_send()
        for copy in send_c(c) + send_y(c):
            copy.wait_send()


def body(queries, new_kv, root_kv, branch_kv, tail_kv, parent, node_len, leaf_of, branch_slot):
    devices = lax.axis_size("kv")
    steps, req_here, _ = queries.shape
    group = QH // KVH
    rows = steps * req_here * group
    depth = devices // 4
    quarter = depth * rows
    chunks = KVH
    slots_here = branch_kv.shape[0]
    block_len = branch_kv.shape[2]

    query = queries.reshape(steps, req_here, KVH, group, HD)
    query = jnp.transpose(query, (2, 0, 1, 3, 4)).reshape(KVH, rows, HD)
    bf, f32 = jnp.bfloat16, jnp.float32
    vmem = pl.BlockSpec(memory_space=pltpu.VMEM)
    smem = pl.BlockSpec(memory_space=pltpu.SMEM)
    hbm = pl.BlockSpec(memory_space=pl.ANY)
    lanes = PAIR * rows
    tokens = (root_kv.shape[0] + slots_here) * block_len
    dma = pltpu.SemaphoreType.DMA
    out = pl.pallas_call(
        functools.partial(kernel, devices, rows, req_here),
        out_shape=jax.ShapeDtypeStruct((chunks, rows, HD), bf),
        in_specs=[smem] * 4 + [vmem] * 2 + [hbm] * 3,
        out_specs=vmem,
        scratch_shapes=[
            pltpu.VMEM((chunks, 2, 2, depth, rows, HD), bf),
            pltpu.VMEM(root_kv.shape, bf),
            pltpu.VMEM(branch_kv.shape, bf),
            pltpu.VMEM(tail_kv.shape, bf),
            pltpu.VMEM((KVH, HD, tokens), bf),
            pltpu.VMEM((2, 2, slots_here, quarter), jnp.int32),
            pltpu.VMEM((req_here, lanes), jnp.int32),
            pltpu.VMEM((2, 16, KVH * HD), bf),
            pltpu.VMEM((chunks, 2, 2, HD, quarter), bf),
            pltpu.VMEM((chunks, 2, 2, 2, quarter), f32),
            pltpu.VMEM((chunks, 2, HD, quarter), bf),
            pltpu.VMEM((chunks, 2, 2, quarter), f32),
            pltpu.VMEM((chunks, 2, HD, quarter), bf),
            pltpu.VMEM((chunks, 2, 2, quarter), f32),
            pltpu.VMEM((chunks, HD, quarter), bf),
            pltpu.VMEM((chunks, 2, quarter), f32),
            pltpu.VMEM((chunks, depth, HD // 2, 2 * rows), bf),
            pltpu.VMEM((chunks, depth, 2, 2 * rows), f32),
            pltpu.VMEM((chunks, depth, HD // 2, 2 * rows), bf),
            pltpu.VMEM((chunks, depth, 2, 2 * rows), f32),
            pltpu.VMEM((chunks, HD // 2, 2 * rows), f32),
            pltpu.VMEM((chunks, 2, 2 * rows), f32),
            dma((3,)),
            dma((chunks, depth)), dma((chunks, depth)),
            dma((chunks,)), dma((chunks,)), dma((chunks,)), dma((chunks,)),
            dma((chunks, 2)), dma((chunks, 2)), dma((chunks, 2)), dma((chunks, 2)),
            dma((chunks, depth, 2)), dma((chunks, depth, 2)),
        ],
        compiler_params=pltpu.CompilerParams(
            collective_id=0, has_side_effects=True, vmem_limit_bytes=56 * 1024 * 1024
        ),
    )(parent, node_len, leaf_of, branch_slot, query, new_kv, root_kv, branch_kv, tail_kv)
    out = out.reshape(KVH, steps, req_here, group, HD)
    return jnp.transpose(out, (1, 2, 0, 3, 4)).reshape(steps, req_here, QH * HD)


def solution(mesh):
    return jax.shard_map(
        body,
        mesh=mesh,
        in_specs=(
            P(None, ("groups", "kv"), None),
            P(None, None, ("groups", "kv"), None),
            P(("groups", "kv"), None, None, None),
            P(("groups", "kv"), None, None, None),
            P(("groups", "kv"), None, None, None),
            P("groups"),
            P("groups"),
            P("groups"),
            P("groups"),
        ),
        out_specs=P(None, ("groups", "kv"), None),
        check_vma=False,
    )
```

```python
import functools

import jax
import jax.numpy as jnp
from jax import lax
from jax.experimental import pallas as pl
from jax.experimental.pallas import tpu as pltpu
from jax.sharding import PartitionSpec as P

QH = 128
KVH = 8
HD = 128
PAIR = 2
MASKED = -1e30
LOG2E = 1.4426950408889634
LAG_Y = 2
LAG_CORE = 3
LAG_OUT_CORE = 4
LAG_OUT_Y = 6
LAG_LAST = 8


def attend(scores):
    unit = HD**-0.5 * LOG2E
    top = functools.reduce(jnp.maximum, [jnp.max(s, axis=0, keepdims=True) for s in scores]) * unit
    weights = [jnp.exp2(s * unit - top) for s in scores]
    total = functools.reduce(jnp.add, [jnp.sum(w, axis=0, keepdims=True) for w in weights])
    return top, total, [w.astype(jnp.bfloat16) for w in weights]


def matmul(a, b, dims):
    return lax.dot_general(a, b, (dims, ((), ())), preferred_element_type=jnp.float32)


def merge(stat_a, out_a, stat_b, out_b):
    top = jnp.maximum(stat_a[0:1], stat_b[0:1])
    wa = stat_a[1:2] * jnp.exp2(stat_a[0:1] - top)
    wb = stat_b[1:2] * jnp.exp2(stat_b[0:1] - top)
    total = wa + wb
    inv = 1.0 / total
    out = out_a.astype(jnp.float32) * (wa * inv) + out_b.astype(jnp.float32) * (wb * inv)
    return jnp.concatenate([top, total], axis=0), out


def kernel(
    devices, rows, req_here,
    parent, node_len, leaf_of, branch_slot,
    q_ref, new_ref, root_hbm, branch_hbm, tail_hbm,
    out_ref,
    qbuf, root, branch, tail, vt, lim_ref, tl_ref, fresh,
    o1, s1, r1, t1, o2, s2, r2, t2, o3, s3, r3, t3, tacc, tst,
    hbm_sem, agz_s, agz_r, agy_s, agy_r, agc_s, agc_r,
    c_s, c_r, y_s, y_r, z_s, z_r,
):
    depth = devices // 4
    chunks = KVH
    half_dim = HD // 2
    group = QH // KVH
    me = lax.axis_index("kv")
    core = lax.rem(me, 2)
    yy = lax.rem(me // 2, 2)
    zz = me // 4
    core_peer = me + 1 - 2 * core
    y_peer = me + 2 - 4 * yy
    n_root = root.shape[0]
    n_branch = branch.shape[0]
    quarter = depth * rows
    steps = new_ref.shape[0]

    def z_peer(offset):
        z = lax.rem(zz + offset, depth)
        return z, z * 4 + yy * 2 + core

    loads = [
        pltpu.make_async_copy(tail_hbm, tail, hbm_sem.at[0]),
        pltpu.make_async_copy(root_hbm, root, hbm_sem.at[1]),
        pltpu.make_async_copy(branch_hbm, branch, hbm_sem.at[2]),
    ]
    for load in loads:
        load.start()

    barrier = pltpu.get_barrier_semaphore()
    for peer in [core_peer, y_peer] + [z_peer(o)[1] for o in range(1, depth)]:
        pl.semaphore_signal(
            barrier, inc=1, device_id={"kv": peer}, device_id_type=pl.DeviceIdType.MESH
        )
    pl.semaphore_wait(barrier, depth + 1)

    def remote(src, dst, send, recv, peer):
        return pltpu.make_async_remote_copy(
            src_ref=src, dst_ref=dst, send_sem=send, recv_sem=recv,
            device_id={"kv": peer}, device_id_type=pl.DeviceIdType.MESH,
        )

    def gather_z(c, o):
        return remote(
            q_ref.at[c], qbuf.at[c, core, yy, zz], agz_s.at[c, o], agz_r.at[c, o], z_peer(o)[1]
        )

    def gather_z_in(c, o):
        z = lax.rem(zz + depth - o, depth)
        return remote(
            q_ref.at[c], qbuf.at[c, core, yy, z], agz_s.at[c, o], agz_r.at[c, o], z_peer(o)[1]
        )

    def gather_y(c, y):
        return remote(qbuf.at[c, core, yy], qbuf.at[c, core, y], agy_s.at[c], agy_r.at[c], y_peer)

    def gather_c(c, half):
        return remote(qbuf.at[c, core], qbuf.at[c, half], agc_s.at[c], agc_r.at[c], core_peer)

    def send_c(c):
        return (
            remote(o1.at[c, 1 - core], r1.at[c], c_s.at[c, 0], c_r.at[c, 0], core_peer),
            remote(s1.at[c, 1 - core], t1.at[c], c_s.at[c, 1], c_r.at[c, 1], core_peer),
        )

    def send_y(c):
        return (
            remote(o2.at[c, 1 - yy], r2.at[c], y_s.at[c, 0], y_r.at[c, 0], y_peer),
            remote(s2.at[c, 1 - yy], t2.at[c], y_s.at[c, 1], y_r.at[c, 1], y_peer),
        )

    def send_z(c, o):
        z, peer = z_peer(o)
        return (
            remote(o3.at[c, z], r3.at[c, o], z_s.at[c, o, 0], z_r.at[c, o, 0], peer),
            remote(s3.at[c, z], t3.at[c, o], z_s.at[c, o, 1], z_r.at[c, o, 1], peer),
        )

    @pl.loop(0, chunks)
    def _(c):
        for o in range(1, depth):
            gather_z(c, o).start()
        qbuf[c, core, yy, zz] = q_ref[c]

    def tables():
        block_len = root.shape[2]
        first_slot = me * n_branch
        slot_nodes = [branch_slot[first_slot + j] for j in range(n_branch)]

        def count_rank(i, ranks):
            node = branch_slot[i]
            return tuple(
                rank + jnp.where((node == slot_nodes[j]) & (i < first_slot + j), 1, 0)
                for j, rank in enumerate(ranks)
            )

        ranks = lax.fori_loop(
            0, branch_slot.shape[0], count_rank, (jnp.int32(0),) * n_branch
        )
        fills = []
        for j in range(n_branch):
            owned = node_len[jnp.minimum(slot_nodes[j], node_len.shape[0] - 1)]
            fill = jnp.clip(owned - ranks[j] * block_len, 0, block_len)
            fills.append(jnp.where(slot_nodes[j] < node_len.shape[0], fill, 0))
        lane = lax.broadcasted_iota(jnp.int32, (1, quarter), 1)
        lane_owner = (lane // rows) * req_here + (lane // group) % req_here
        for half in range(2):
            for y in range(2):
                lane_branch = jnp.zeros((1, quarter), jnp.int32)
                for z in range(depth):
                    for r in range(req_here):
                        request = ((z * 2 + y) * 2 + half) * req_here + r
                        lane_branch = jnp.where(
                            lane_owner == z * req_here + r, parent[leaf_of[request]], lane_branch
                        )
                for j in range(n_branch):
                    lim_ref[half, y, j : j + 1, :] = jnp.where(
                        lane_branch == slot_nodes[j], fills[j], 0
                    )
        lane = lax.broadcasted_iota(jnp.int32, (1, PAIR * rows), 1)
        for r in range(req_here):
            tl_ref[r : r + 1, :] = jnp.where(
                (lane // group) % req_here == r, node_len[leaf_of[me * req_here + r]], 0
            )
        fresh[...] = jnp.zeros_like(fresh)
        for s in range(steps):
            for kv in range(2):
                fresh[kv, s * req_here : (s + 1) * req_here, :] = new_ref[s, kv]

    def head_cols(k):
        return pl.ds(pl.multiple_of(k * HD, HD), HD)

    def fold(x, part):
        return jnp.concatenate([x[:half_dim, part], x[half_dim:, part]], axis=1)

    def tail_part(c):
        query = [q_ref[c * PAIR + h] for h in range(PAIR)]
        cols = [head_cols(c * PAIR + h) for h in range(PAIR)]
        scores = []
        for r in range(req_here):
            s = jnp.concatenate(
                [matmul(tail[r, 0, :, cols[h]], query[h], ((1,), (1,))) for h in range(PAIR)], axis=1
            )
            token = lax.broadcasted_iota(jnp.int32, s.shape, 0)
            scores.append(jnp.where(token < tl_ref[r : r + 1, :], s, MASKED))
        s = jnp.concatenate(
            [matmul(fresh[0, :, cols[h]], query[h], ((1,), (1,))) for h in range(PAIR)], axis=1
        )
        token = lax.broadcasted_iota(jnp.int32, s.shape, 0)
        lane = lax.broadcasted_iota(jnp.int32, s.shape, 1)
        lane_req = (lane // group) % req_here
        lane_step = (lane // (group * req_here)) % steps
        live = (token < steps * req_here) & (token % req_here == lane_req)
        live = live & (token // req_here <= lane_step)
        scores.append(jnp.where(live, s, MASKED))
        top, total, weights = attend(scores)
        outs = []
        for h in range(PAIR):
            values = [tail[r, 1, :, cols[h]] for r in range(req_here)] + [fresh[1, :, cols[h]]]
            outs.append(
                functools.reduce(
                    jnp.add, [matmul(v, w, ((0,), (0,))) for v, w in zip(values, weights)]
                )
            )
        stat = jnp.concatenate([top, total], axis=0)
        for h in range(PAIR):
            part = slice(h * rows, (h + 1) * rows)
            tacc[c * PAIR + h] = fold(outs[h], part)
            tst[c * PAIR + h] = jnp.concatenate([stat[:, part]] * 2, axis=1)

    def cache_part(c, half):
        @pl.loop(0, 2)
        def _(y):
            cols = head_cols(c)
            query = qbuf[c, half, y].reshape(quarter, HD)
            scores = [matmul(root[b, 0, :, cols], query, ((1,), (1,))) for b in range(n_root)]
            for b in range(n_branch):
                s = matmul(branch[b, 0, :, cols], query, ((1,), (1,)))
                token = lax.broadcasted_iota(jnp.int32, s.shape, 0)
                scores.append(jnp.where(token < lim_ref[half, y, b : b + 1, :], s, MASKED))
            top, total, weights = attend(scores)
            out = matmul(vt[c], jnp.concatenate(weights, axis=0), ((1,), (0,)))
            o1[c, half, y] = (out * (1.0 / total)).astype(jnp.bfloat16)
            s1[c, half, y] = jnp.concatenate([top, total], axis=0)

    def turn_values(k):
        cols = head_cols(k)
        for b in range(n_root):
            vt[k, :, b * HD : (b + 1) * HD] = root[b, 1, :, cols].T
        for b in range(n_branch):
            vt[k, :, (n_root + b) * HD : (n_root + b + 1) * HD] = branch[b, 1, :, cols].T

    @pl.loop(0, chunks + LAG_LAST)
    def _(t):
        @pl.when(t < chunks)
        def _():
            for o in range(1, depth):
                gather_z_in(t, o).wait_recv()
            gather_y(t, yy).start()

        @pl.when((t >= LAG_Y) & (t < chunks + LAG_Y))
        def _():
            c = t - LAG_Y
            gather_y(c, 1 - yy).wait_recv()
            gather_c(c, core).start()

        @pl.when(t == 0)
        def _():
            tables()
            for load in loads:
                load.wait()

        @pl.when(t < chunks // PAIR)
        def _():
            turn_values(PAIR * t)
            turn_values(PAIR * t + 1)
            tail_part(t)

        @pl.when((t >= LAG_CORE) & (t < chunks + LAG_CORE))
        def _():
            c = t - LAG_CORE
            gather_c(c, 1 - core).wait_recv()
            cache_part(c, 1 - core)
            for copy in send_c(c):
                copy.start()
            cache_part(c, core)

        @pl.when((t >= LAG_OUT_CORE) & (t < chunks + LAG_OUT_CORE))
        def _():
            c = t - LAG_OUT_CORE
            for copy in send_c(c):
                copy.wait_recv()
            for y in range(2):
                stat, out = merge(s1[c, core, y], o1[c, core, y], t1[c, y], r1[c, y])
                o2[c, y] = out.astype(jnp.bfloat16)
                s2[c, y] = stat
            for copy in send_y(c):
                copy.start()

        @pl.when((t >= LAG_OUT_Y) & (t < chunks + LAG_OUT_Y))
        def _():
            c = t - LAG_OUT_Y
            for copy in send_y(c):
                copy.wait_recv()
            stat, out = merge(s2[c, yy], o2[c, yy], t2[c], r2[c])
            for z in range(depth):
                part = slice(z * rows, (z + 1) * rows)
                o3[c, z] = fold(out, part).astype(jnp.bfloat16)
                s3[c, z] = jnp.concatenate([stat[:, part]] * 2, axis=1)
            for o in range(1, depth):
                for copy in send_z(c, o):
                    copy.start()

        @pl.when(t >= LAG_LAST)
        def _():
            c = t - LAG_LAST
            for o in range(1, depth):
                for copy in send_z(c, o):
                    copy.wait_recv()
            stats = [s3[c, zz]] + [t3[c, o] for o in range(1, depth)]
            outs = [o3[c, zz]] + [r3[c, o] for o in range(1, depth)]
            own = tst[c]
            top = functools.reduce(jnp.maximum, [s[0:1] for s in stats] + [own[0:1]])
            scale = jnp.exp2(own[0:1] - top)
            number = tacc[c] * scale
            total = own[1:2] * scale
            for s, o in zip(stats, outs):
                factor = s[1:2] * jnp.exp2(s[0:1] - top)
                number = number + o.astype(jnp.float32) * factor
                total = total + factor
            out = number / total
            out = jnp.concatenate([out[:, :rows], out[:, rows:]], axis=0)
            out_ref[c] = out.T.astype(jnp.bfloat16)

    @pl.loop(0, chunks)
    def _(c):
        for o in range(1, depth):
            gather_z(c, o).wait_send()
            for copy in send_z(c, o):
                copy.wait_send()
        gather_y(c, yy).wait_send()
        gather_c(c, core).wait_send()
        for copy in send_c(c) + send_y(c):
            copy.wait_send()


def body(queries, new_kv, root_kv, branch_kv, tail_kv, parent, node_len, leaf_of, branch_slot):
    devices = lax.axis_size("kv")
    steps, req_here, _ = queries.shape
    group = QH // KVH
    rows = steps * req_here * group
    depth = devices // 4
    quarter = depth * rows
    chunks = KVH
    slots_here = branch_kv.shape[0]
    block_len = branch_kv.shape[2]

    query = queries.reshape(steps, req_here, KVH, group, HD)
    query = jnp.transpose(query, (2, 0, 1, 3, 4)).reshape(KVH, rows, HD)
    bf, f32 = jnp.bfloat16, jnp.float32
    vmem = pl.BlockSpec(memory_space=pltpu.VMEM)
    smem = pl.BlockSpec(memory_space=pltpu.SMEM)
    hbm = pl.BlockSpec(memory_space=pl.ANY)
    lanes = PAIR * rows
    tokens = (root_kv.shape[0] + slots_here) * block_len
    dma = pltpu.SemaphoreType.DMA
    out = pl.pallas_call(
        functools.partial(kernel, devices, rows, req_here),
        out_shape=jax.ShapeDtypeStruct((chunks, rows, HD), bf),
        in_specs=[smem] * 4 + [vmem] * 2 + [hbm] * 3,
        out_specs=vmem,
        scratch_shapes=[
            pltpu.VMEM((chunks, 2, 2, depth, rows, HD), bf),
            pltpu.VMEM(root_kv.shape, bf),
            pltpu.VMEM(branch_kv.shape, bf),
            pltpu.VMEM(tail_kv.shape, bf),
            pltpu.VMEM((KVH, HD, tokens), bf),
            pltpu.VMEM((2, 2, slots_here, quarter), jnp.int32),
            pltpu.VMEM((req_here, lanes), jnp.int32),
            pltpu.VMEM((2, 16, KVH * HD), bf),
            pltpu.VMEM((chunks, 2, 2, HD, quarter), bf),
            pltpu.VMEM((chunks, 2, 2, 2, quarter), f32),
            pltpu.VMEM((chunks, 2, HD, quarter), bf),
            pltpu.VMEM((chunks, 2, 2, quarter), f32),
            pltpu.VMEM((chunks, 2, HD, quarter), bf),
            pltpu.VMEM((chunks, 2, 2, quarter), f32),
            pltpu.VMEM((chunks, HD, quarter), bf),
            pltpu.VMEM((chunks, 2, quarter), f32),
            pltpu.VMEM((chunks, depth, HD // 2, 2 * rows), bf),
            pltpu.VMEM((chunks, depth, 2, 2 * rows), f32),
            pltpu.VMEM((chunks, depth, HD // 2, 2 * rows), bf),
            pltpu.VMEM((chunks, depth, 2, 2 * rows), f32),
            pltpu.VMEM((chunks, HD // 2, 2 * rows), f32),
            pltpu.VMEM((chunks, 2, 2 * rows), f32),
            dma((3,)),
            dma((chunks, depth)), dma((chunks, depth)),
            dma((chunks,)), dma((chunks,)), dma((chunks,)), dma((chunks,)),
            dma((chunks, 2)), dma((chunks, 2)), dma((chunks, 2)), dma((chunks, 2)),
            dma((chunks, depth, 2)), dma((chunks, depth, 2)),
        ],
        compiler_params=pltpu.CompilerParams(
            collective_id=0, has_side_effects=True, vmem_limit_bytes=56 * 1024 * 1024
        ),
    )(parent, node_len, leaf_of, branch_slot, query, new_kv, root_kv, branch_kv, tail_kv)
    out = out.reshape(KVH, steps, req_here, group, HD)
    return jnp.transpose(out, (1, 2, 0, 3, 4)).reshape(steps, req_here, QH * HD)


def solution(mesh):
    return jax.shard_map(
        body,
        mesh=mesh,
        in_specs=(
            P(None, ("groups", "kv"), None),
            P(None, None, ("groups", "kv"), None),
            P(("groups", "kv"), None, None, None),
            P(("groups", "kv"), None, None, None),
            P(("groups", "kv"), None, None, None),
            P("groups"),
            P("groups"),
            P("groups"),
            P("groups"),
        ),
        out_specs=P(None, ("groups", "kv"), None),
        check_vma=False,
    )
```

```python
import functools

import jax
import jax.numpy as jnp
from jax import lax
from jax.experimental import pallas as pl
from jax.experimental.pallas import tpu as pltpu
from jax.sharding import PartitionSpec as P

QH = 128
KVH = 8
HD = 128
PAIR = 2
MASKED = -1e30
LOG2E = 1.4426950408889634
LAG_Y = 2
LAG_CORE = 3
LAG_OUT_CORE = 4
LAG_OUT_Y = 6
LAG_LAST = 8


def attend(scores):
    unit = HD**-0.5 * LOG2E
    top = functools.reduce(jnp.maximum, [jnp.max(s, axis=0, keepdims=True) for s in scores]) * unit
    weights = [jnp.exp2(s * unit - top) for s in scores]
    total = functools.reduce(jnp.add, [jnp.sum(w, axis=0, keepdims=True) for w in weights])
    return top, total, [w.astype(jnp.bfloat16) for w in weights]


def matmul(a, b, dims):
    return lax.dot_general(a, b, (dims, ((), ())), preferred_element_type=jnp.float32)


def merge(stat_a, out_a, stat_b, out_b):
    top = jnp.maximum(stat_a[0:1], stat_b[0:1])
    wa = stat_a[1:2] * jnp.exp2(stat_a[0:1] - top)
    wb = stat_b[1:2] * jnp.exp2(stat_b[0:1] - top)
    total = wa + wb
    inv = 1.0 / total
    out = out_a.astype(jnp.float32) * (wa * inv) + out_b.astype(jnp.float32) * (wb * inv)
    return jnp.concatenate([top, total], axis=0), out


def kernel(
    devices, rows, req_here,
    parent, node_len, leaf_of, branch_slot,
    q_ref, new_ref, root_hbm, branch_hbm, tail_hbm,
    out_ref,
    qbuf, root, branch, tail, vt, lim_ref, tl_ref, fresh,
    o1, s1, r1, t1, o2, s2, r2, t2, o3, s3, r3, t3, tacc, tst,
    hbm_sem, agz_s, agz_r, agy_s, agy_r, agc_s, agc_r,
    c_s, c_r, y_s, y_r, z_s, z_r,
):
    depth = devices // 4
    chunks = KVH
    half_dim = HD // 2
    group = QH // KVH
    me = lax.axis_index("kv")
    core = lax.rem(me, 2)
    yy = lax.rem(me // 2, 2)
    zz = me // 4
    core_peer = me + 1 - 2 * core
    y_peer = me + 2 - 4 * yy
    n_root = root.shape[0]
    n_branch = branch.shape[0]
    quarter = depth * rows
    steps = new_ref.shape[0]

    def z_peer(offset):
        z = lax.rem(zz + offset, depth)
        return z, z * 4 + yy * 2 + core

    loads = [
        pltpu.make_async_copy(tail_hbm, tail, hbm_sem.at[0]),
        pltpu.make_async_copy(root_hbm, root, hbm_sem.at[1]),
        pltpu.make_async_copy(branch_hbm, branch, hbm_sem.at[2]),
    ]
    for load in loads:
        load.start()

    barrier = pltpu.get_barrier_semaphore()
    for peer in [core_peer, y_peer] + [z_peer(o)[1] for o in range(1, depth)]:
        pl.semaphore_signal(
            barrier, inc=1, device_id={"kv": peer}, device_id_type=pl.DeviceIdType.MESH
        )
    pl.semaphore_wait(barrier, depth + 1)

    def remote(src, dst, send, recv, peer):
        return pltpu.make_async_remote_copy(
            src_ref=src, dst_ref=dst, send_sem=send, recv_sem=recv,
            device_id={"kv": peer}, device_id_type=pl.DeviceIdType.MESH,
        )

    def gather_z(c, o):
        return remote(
            q_ref.at[c], qbuf.at[c, core, yy, zz], agz_s.at[c, o], agz_r.at[c, o], z_peer(o)[1]
        )

    def gather_z_in(c, o):
        z = lax.rem(zz + depth - o, depth)
        return remote(
            q_ref.at[c], qbuf.at[c, core, yy, z], agz_s.at[c, o], agz_r.at[c, o], z_peer(o)[1]
        )

    def gather_y(c, y):
        return remote(qbuf.at[c, core, yy], qbuf.at[c, core, y], agy_s.at[c], agy_r.at[c], y_peer)

    def gather_c(c, half):
        return remote(qbuf.at[c, core], qbuf.at[c, half], agc_s.at[c], agc_r.at[c], core_peer)

    def send_c(c):
        return (
            remote(o1.at[c, 1 - core], r1.at[c], c_s.at[c, 0], c_r.at[c, 0], core_peer),
            remote(s1.at[c, 1 - core], t1.at[c], c_s.at[c, 1], c_r.at[c, 1], core_peer),
        )

    def send_y(c):
        return (
            remote(o2.at[c, 1 - yy], r2.at[c], y_s.at[c, 0], y_r.at[c, 0], y_peer),
            remote(s2.at[c, 1 - yy], t2.at[c], y_s.at[c, 1], y_r.at[c, 1], y_peer),
        )

    def send_z(c, o):
        z, peer = z_peer(o)
        return (
            remote(o3.at[c, z], r3.at[c, o], z_s.at[c, o, 0], z_r.at[c, o, 0], peer),
            remote(s3.at[c, z], t3.at[c, o], z_s.at[c, o, 1], z_r.at[c, o, 1], peer),
        )

    @pl.loop(0, chunks)
    def _(c):
        for o in range(1, depth):
            gather_z(c, o).start()
        qbuf[c, core, yy, zz] = q_ref[c]

    def tables():
        block_len = root.shape[2]
        first_slot = me * n_branch
        slot_nodes = [branch_slot[first_slot + j] for j in range(n_branch)]

        def count_rank(i, ranks):
            node = branch_slot[i]
            return tuple(
                rank + jnp.where((node == slot_nodes[j]) & (i < first_slot + j), 1, 0)
                for j, rank in enumerate(ranks)
            )

        ranks = lax.fori_loop(
            0, branch_slot.shape[0], count_rank, (jnp.int32(0),) * n_branch
        )
        fills = []
        for j in range(n_branch):
            owned = node_len[jnp.minimum(slot_nodes[j], node_len.shape[0] - 1)]
            fill = jnp.clip(owned - ranks[j] * block_len, 0, block_len)
            fills.append(jnp.where(slot_nodes[j] < node_len.shape[0], fill, 0))
        lane = lax.broadcasted_iota(jnp.int32, (1, quarter), 1)
        lane_owner = (lane // rows) * req_here + (lane // group) % req_here
        for half in range(2):
            for y in range(2):
                lane_branch = jnp.zeros((1, quarter), jnp.int32)
                for z in range(depth):
                    for r in range(req_here):
                        request = ((z * 2 + y) * 2 + half) * req_here + r
                        lane_branch = jnp.where(
                            lane_owner == z * req_here + r, parent[leaf_of[request]], lane_branch
                        )
                for j in range(n_branch):
                    lim_ref[half, y, j : j + 1, :] = jnp.where(
                        lane_branch == slot_nodes[j], fills[j], 0
                    )
        lane = lax.broadcasted_iota(jnp.int32, (1, PAIR * rows), 1)
        for r in range(req_here):
            tl_ref[r : r + 1, :] = jnp.where(
                (lane // group) % req_here == r, node_len[leaf_of[me * req_here + r]], 0
            )
        fresh[...] = jnp.zeros_like(fresh)
        for s in range(steps):
            for kv in range(2):
                fresh[kv, s * req_here : (s + 1) * req_here, :] = new_ref[s, kv]

    def head_cols(k):
        return pl.ds(pl.multiple_of(k * HD, HD), HD)

    def fold(x, part):
        return jnp.concatenate([x[:half_dim, part], x[half_dim:, part]], axis=1)

    def tail_part(c):
        query = [q_ref[c * PAIR + h] for h in range(PAIR)]
        cols = [head_cols(c * PAIR + h) for h in range(PAIR)]
        scores = []
        for r in range(req_here):
            s = jnp.concatenate(
                [matmul(tail[r, 0, :, cols[h]], query[h], ((1,), (1,))) for h in range(PAIR)], axis=1
            )
            token = lax.broadcasted_iota(jnp.int32, s.shape, 0)
            scores.append(jnp.where(token < tl_ref[r : r + 1, :], s, MASKED))
        s = jnp.concatenate(
            [matmul(fresh[0, :, cols[h]], query[h], ((1,), (1,))) for h in range(PAIR)], axis=1
        )
        token = lax.broadcasted_iota(jnp.int32, s.shape, 0)
        lane = lax.broadcasted_iota(jnp.int32, s.shape, 1)
        lane_req = (lane // group) % req_here
        lane_step = (lane // (group * req_here)) % steps
        live = (token < steps * req_here) & (token % req_here == lane_req)
        live = live & (token // req_here <= lane_step)
        scores.append(jnp.where(live, s, MASKED))
        top, total, weights = attend(scores)
        outs = []
        for h in range(PAIR):
            values = [tail[r, 1, :, cols[h]] for r in range(req_here)] + [fresh[1, :, cols[h]]]
            outs.append(
                functools.reduce(
                    jnp.add, [matmul(v, w, ((0,), (0,))) for v, w in zip(values, weights)]
                )
            )
        stat = jnp.concatenate([top, total], axis=0)
        for h in range(PAIR):
            part = slice(h * rows, (h + 1) * rows)
            tacc[c * PAIR + h] = fold(outs[h], part)
            tst[c * PAIR + h] = jnp.concatenate([stat[:, part]] * 2, axis=1)

    def cache_part(c, half):
        @pl.loop(0, 2, unroll=True)
        def _(y):
            cols = head_cols(c)
            query = qbuf[c, half, y].reshape(quarter, HD)
            scores = [matmul(root[b, 0, :, cols], query, ((1,), (1,))) for b in range(n_root)]
            for b in range(n_branch):
                s = matmul(branch[b, 0, :, cols], query, ((1,), (1,)))
                token = lax.broadcasted_iota(jnp.int32, s.shape, 0)
                scores.append(jnp.where(token < lim_ref[half, y, b : b + 1, :], s, MASKED))
            top, total, weights = attend(scores)
            out = matmul(vt[c], jnp.concatenate(weights, axis=0), ((1,), (0,)))
            o1[c, half, y] = (out * (1.0 / total)).astype(jnp.bfloat16)
            s1[c, half, y] = jnp.concatenate([top, total], axis=0)

    def turn_values(k):
        cols = head_cols(k)
        for b in range(n_root):
            vt[k, :, b * HD : (b + 1) * HD] = root[b, 1, :, cols].T
        for b in range(n_branch):
            vt[k, :, (n_root + b) * HD : (n_root + b + 1) * HD] = branch[b, 1, :, cols].T

    @pl.loop(0, chunks + LAG_LAST)
    def _(t):
        @pl.when(t < chunks)
        def _():
            for o in range(1, depth):
                gather_z_in(t, o).wait_recv()
            gather_y(t, yy).start()

        @pl.when((t >= LAG_Y) & (t < chunks + LAG_Y))
        def _():
            c = t - LAG_Y
            gather_y(c, 1 - yy).wait_recv()
            gather_c(c, core).start()

        @pl.when(t == 0)
        def _():
            tables()
            for load in loads:
                load.wait()

        @pl.when(t < chunks // PAIR)
        def _():
            turn_values(PAIR * t)
            turn_values(PAIR * t + 1)
            tail_part(t)

        @pl.when((t >= LAG_CORE) & (t < chunks + LAG_CORE))
        def _():
            c = t - LAG_CORE
            gather_c(c, 1 - core).wait_recv()
            cache_part(c, 1 - core)
            for copy in send_c(c):
                copy.start()
            cache_part(c, core)

        @pl.when((t >= LAG_OUT_CORE) & (t < chunks + LAG_OUT_CORE))
        def _():
            c = t - LAG_OUT_CORE
            for copy in send_c(c):
                copy.wait_recv()
            for y in range(2):
                stat, out = merge(s1[c, core, y], o1[c, core, y], t1[c, y], r1[c, y])
                o2[c, y] = out.astype(jnp.bfloat16)
                s2[c, y] = stat
            for copy in send_y(c):
                copy.start()

        @pl.when((t >= LAG_OUT_Y) & (t < chunks + LAG_OUT_Y))
        def _():
            c = t - LAG_OUT_Y
            for copy in send_y(c):
                copy.wait_recv()
            stat, out = merge(s2[c, yy], o2[c, yy], t2[c], r2[c])
            for z in range(depth):
                part = slice(z * rows, (z + 1) * rows)
                o3[c, z] = fold(out, part).astype(jnp.bfloat16)
                s3[c, z] = jnp.concatenate([stat[:, part]] * 2, axis=1)
            for o in range(1, depth):
                for copy in send_z(c, o):
                    copy.start()

        @pl.when(t >= LAG_LAST)
        def _():
            c = t - LAG_LAST
            for o in range(1, depth):
                for copy in send_z(c, o):
                    copy.wait_recv()
            stats = [s3[c, zz]] + [t3[c, o] for o in range(1, depth)]
            outs = [o3[c, zz]] + [r3[c, o] for o in range(1, depth)]
            own = tst[c]
            top = functools.reduce(jnp.maximum, [s[0:1] for s in stats] + [own[0:1]])
            scale = jnp.exp2(own[0:1] - top)
            number = tacc[c] * scale
            total = own[1:2] * scale
            for s, o in zip(stats, outs):
                factor = s[1:2] * jnp.exp2(s[0:1] - top)
                number = number + o.astype(jnp.float32) * factor
                total = total + factor
            out = number / total
            out = jnp.concatenate([out[:, :rows], out[:, rows:]], axis=0)
            out_ref[c] = out.T.astype(jnp.bfloat16)

    @pl.loop(0, chunks)
    def _(c):
        for o in range(1, depth):
            gather_z(c, o).wait_send()
            for copy in send_z(c, o):
                copy.wait_send()
        gather_y(c, yy).wait_send()
        gather_c(c, core).wait_send()
        for copy in send_c(c) + send_y(c):
            copy.wait_send()


def body(queries, new_kv, root_kv, branch_kv, tail_kv, parent, node_len, leaf_of, branch_slot):
    devices = lax.axis_size("kv")
    steps, req_here, _ = queries.shape
    group = QH // KVH
    rows = steps * req_here * group
    depth = devices // 4
    quarter = depth * rows
    chunks = KVH
    slots_here = branch_kv.shape[0]
    block_len = branch_kv.shape[2]

    query = queries.reshape(steps, req_here, KVH, group, HD)
    query = jnp.transpose(query, (2, 0, 1, 3, 4)).reshape(KVH, rows, HD)
    bf, f32 = jnp.bfloat16, jnp.float32
    vmem = pl.BlockSpec(memory_space=pltpu.VMEM)
    smem = pl.BlockSpec(memory_space=pltpu.SMEM)
    hbm = pl.BlockSpec(memory_space=pl.ANY)
    lanes = PAIR * rows
    tokens = (root_kv.shape[0] + slots_here) * block_len
    dma = pltpu.SemaphoreType.DMA
    out = pl.pallas_call(
        functools.partial(kernel, devices, rows, req_here),
        out_shape=jax.ShapeDtypeStruct((chunks, rows, HD), bf),
        in_specs=[smem] * 4 + [vmem] * 2 + [hbm] * 3,
        out_specs=vmem,
        scratch_shapes=[
            pltpu.VMEM((chunks, 2, 2, depth, rows, HD), bf),
            pltpu.VMEM(root_kv.shape, bf),
            pltpu.VMEM(branch_kv.shape, bf),
            pltpu.VMEM(tail_kv.shape, bf),
            pltpu.VMEM((KVH, HD, tokens), bf),
            pltpu.VMEM((2, 2, slots_here, quarter), jnp.int32),
            pltpu.VMEM((req_here, lanes), jnp.int32),
            pltpu.VMEM((2, 16, KVH * HD), bf),
            pltpu.VMEM((chunks, 2, 2, HD, quarter), bf),
            pltpu.VMEM((chunks, 2, 2, 2, quarter), f32),
            pltpu.VMEM((chunks, 2, HD, quarter), bf),
            pltpu.VMEM((chunks, 2, 2, quarter), f32),
            pltpu.VMEM((chunks, 2, HD, quarter), bf),
            pltpu.VMEM((chunks, 2, 2, quarter), f32),
            pltpu.VMEM((chunks, HD, quarter), bf),
            pltpu.VMEM((chunks, 2, quarter), f32),
            pltpu.VMEM((chunks, depth, HD // 2, 2 * rows), bf),
            pltpu.VMEM((chunks, depth, 2, 2 * rows), f32),
            pltpu.VMEM((chunks, depth, HD // 2, 2 * rows), bf),
            pltpu.VMEM((chunks, depth, 2, 2 * rows), f32),
            pltpu.VMEM((chunks, HD // 2, 2 * rows), f32),
            pltpu.VMEM((chunks, 2, 2 * rows), f32),
            dma((3,)),
            dma((chunks, depth)), dma((chunks, depth)),
            dma((chunks,)), dma((chunks,)), dma((chunks,)), dma((chunks,)),
            dma((chunks, 2)), dma((chunks, 2)), dma((chunks, 2)), dma((chunks, 2)),
            dma((chunks, depth, 2)), dma((chunks, depth, 2)),
        ],
        compiler_params=pltpu.CompilerParams(
            collective_id=0, has_side_effects=True, vmem_limit_bytes=56 * 1024 * 1024
        ),
    )(parent, node_len, leaf_of, branch_slot, query, new_kv, root_kv, branch_kv, tail_kv)
    out = out.reshape(KVH, steps, req_here, group, HD)
    return jnp.transpose(out, (1, 2, 0, 3, 4)).reshape(steps, req_here, QH * HD)


def solution(mesh):
    return jax.shard_map(
        body,
        mesh=mesh,
        in_specs=(
            P(None, ("groups", "kv"), None),
            P(None, None, ("groups", "kv"), None),
            P(("groups", "kv"), None, None, None),
            P(("groups", "kv"), None, None, None),
            P(("groups", "kv"), None, None, None),
            P("groups"),
            P("groups"),
            P("groups"),
            P("groups"),
        ),
        out_specs=P(None, ("groups", "kv"), None),
        check_vma=False,
    )
```
